32 devices in a mesh: dp: 4 (over y, core), row: 2 (over x), col: 4 (over z).
Axes of the slice: x: 2, y: 2, z: 4, core: 2. Of those that a mesh axis runs over, the one named last changes fastest.
Arguments:
- tokens: bfloat16 [16384, 1152], P(('dp', 'col')), may hold values from -6 to 6
- segment_ids: int32 [16384], P(('dp', 'col')), may hold values from -1 to 10, as said below
- doc_starts: int32 [4, 12], P('dp'), may hold values from 0 to 4096, as said below
- norm1_gain: bfloat16 [1152], P('col'), may hold values from 0.25 to 1.75
- norm2_gain: bfloat16 [1152], P('col'), may hold values from 0.25 to 1.75
- query_key_value_weight: bfloat16 [1152, 6, 320], P('col', 'row'), may hold values from -0.1875 to 0.1875
- output_weight: bfloat16 [1152, 6, 192], P('col', 'row'), may hold values from -2 to 2
- w_gate_up: bfloat16 [1152, 2, 3072], P('col', None, 'row'), may hold values from -0.1875 to 0.1875
- w_down: bfloat16 [1152, 3072], P('col', 'row'), may hold values from -0.21875 to 0.21875
- cotangent: bfloat16 [16384, 1152], P(('dp', 'col')), may hold values from -6 to 6
Outputs:
- layer_output: bfloat16 [16384, 1152], P(('dp', 'col'))
- input_grad: float32 [16384, 1152], P(('dp', 'col'))
- norm1_gain_grad: float32 [1152], P('col')
- norm2_gain_grad: float32 [1152], P('col')
- w_qkv_grad: float32 [1152, 6, 320], P('col', 'row')
- w_out_grad: float32 [1152, 6, 192], P('col', 'row')
- w_gate_up_grad: float32 [1152, 2, 3072], P('col', None, 'row')
- w_down_grad: float32 [1152, 3072], P('col', 'row')
The draws below stay inside these ranges and needn't reach their ends.
Inputs may be any that keep to these rules, and one draw needn't show every extreme that they name: `segment_ids`: each sequence of 4096 tokens is a run of whole documents numbered 0, 1, 2, ... in order, each of 200 to 2000 tokens, the first exactly 2000, followed by at least one padding token with segment -1. doc_starts[s, d] is the index within sequence s of the first token of its document d; slots after its last document hold 4096.
All inputs are finite; a program needn't handle non-finite values.
Results may differ from the reference program's by a relative error of at most 0.014.
Values may be sent and summed in bfloat16 or wider, within the bound.
No kernel may reach another device: no remote copies, remote signals or barrier semaphores. Data moves between devices by JAX's collectives and lax.ppermute only.
A program may use at most 192 MiB of HBM per device.

```python
import math
import jax
import jax.numpy as jnp
from jax import lax

MODEL_WIDTH = 1152
QUERY_HEADS = 18
KEY_VALUE_HEADS = 6
HEAD_WIDTH = 64
FF = 3072
GROUP_QUERIES = 3
SEQUENCE_TOKENS = 4096
DOC_MOST = 2000
DOC_LEAST = 200
DOCS = 12
TOKENS = 16384


def doc_layout(key):
    seq_count = TOKENS // SEQUENCE_TOKENS
    layout_key = jax.random.fold_in(key, 11)
    length_key, pad_key = jax.random.split(layout_key)
    lengths = jax.random.randint(length_key, (seq_count, DOCS), DOC_LEAST, DOC_MOST + 1)
    slot_index = jnp.arange(DOCS, dtype=jnp.int32)[None, :]
    first_row = (jnp.arange(seq_count, dtype=jnp.int32) == 0)[:, None]
    lengths = jnp.where(first_row, DOC_LEAST, lengths)
    lengths = jnp.where(slot_index == 0, DOC_MOST, lengths).astype(jnp.int32)
    most_docs = (SEQUENCE_TOKENS - DOC_MOST - 1) // DOC_LEAST
    padding = jax.random.randint(pad_key, (seq_count, 1), 1, 5).astype(jnp.int32)
    padding = jnp.where(first_row, SEQUENCE_TOKENS - DOC_MOST - most_docs * DOC_LEAST, padding).astype(jnp.int32)
    usable = SEQUENCE_TOKENS - padding
    doc_ends = jnp.cumsum(lengths, axis=1)
    doc_begin = doc_ends - lengths
    doc_kept = doc_begin + DOC_LEAST <= usable
    last_end = jnp.max(jnp.where(doc_kept, jnp.minimum(doc_ends, usable), 0), axis=1)
    start_table = jnp.where(doc_kept, doc_begin, SEQUENCE_TOKENS).astype(jnp.int32)
    token_positions = jnp.arange(SEQUENCE_TOKENS, dtype=jnp.int32)
    started = start_table[:, None, :] <= token_positions[None, :, None]
    counted = jnp.sum(started.astype(jnp.int32), axis=2) - 1
    segments = jnp.where(token_positions[None, :] < last_end[:, None], counted, -1)
    return (start_table, segments.reshape(seq_count * SEQUENCE_TOKENS).astype(jnp.int32))


def draw_segment_ids(key, part):
    return doc_layout(key)[1]


def draw_doc_starts(key, part):
    return doc_layout(key)[0]


def with_spikes(drawn, own_key, source, target, parts, factor):
    def block_of(axis_at):
        return (jnp.arange(drawn.shape[axis_at]) // (drawn.shape[axis_at] // parts)).reshape((-1,) + (1,) * (drawn.ndim - 1 - axis_at))

    one_side = jax.random.permutation(own_key, parts)[block_of(target)]
    far = (block_of(target) + parts // 2) % parts
    return jnp.where((block_of(source) == one_side) | (block_of(source) == far), factor * drawn, drawn)


def level_of(rng, extent, cuts, least, top_value):
    def one(axis_at, blocks):
        steps = jax.random.uniform(jax.random.fold_in(jax.random.fold_in(rng, 6), axis_at), (blocks,), jnp.float32, least / len(cuts), top_value / len(cuts))
        return jnp.repeat(jnp.exp(steps), extent[axis_at] // blocks).reshape((-1,) + (1,) * (len(extent) - axis_at - 1))

    level = one(*cuts[0])
    for cut in cuts[1:]:
        level = level * one(*cut)
    return level


def bell_draw(rng, shape, deviation, bound, cuts=(), kind=jnp.bfloat16):
    factor_of = level_of(rng, shape, cuts, -0.22, 0.18) if cuts else 1.0
    values = jax.random.normal(rng, shape, jnp.float32) * deviation * factor_of
    return jnp.minimum(jnp.maximum(values, -bound), bound).astype(kind)


def gaussian_with(rng, dims, scale, reach, shards, heavy, kind=jnp.bfloat16):
    values = scale * jax.random.normal(rng, dims, jnp.float32)
    if shards:
        values = values * level_of(rng, dims, shards, -0.22, 0.18)
    return jnp.clip(with_spikes(values, jax.random.fold_in(rng, 3), *heavy), -reach, reach).astype(kind)


def setup_inputs(seed: int = 0) -> dict:
    splits = jax.random.split(jax.random.key(seed), 11)
    return {
        "tokens": bell_draw(splits[0], (TOKENS, MODEL_WIDTH), 1.0, 6.0, ((0, 16),)),
        "segment_ids": draw_segment_ids(jax.random.fold_in(splits[10], 71), 0),
        "doc_starts": draw_doc_starts(jax.random.fold_in(splits[10], 71), 0),
        "norm1_gain": jnp.clip(1.0 + 0.15 * jax.random.normal(splits[3], (MODEL_WIDTH,), jnp.float32), 0.25, 1.75).astype(jnp.bfloat16),
        "norm2_gain": jnp.clip(1.0 + 0.15 * jax.random.normal(splits[4], (MODEL_WIDTH,), jnp.float32), 0.25, 1.75).astype(jnp.bfloat16),
        "query_key_value_weight": bell_draw(splits[5], (MODEL_WIDTH, KEY_VALUE_HEADS, (GROUP_QUERIES + 2) * HEAD_WIDTH), MODEL_WIDTH ** -0.5, 0.1875, ((0, 4), (1, 2))),
        "output_weight": bell_draw(splits[6], (MODEL_WIDTH, KEY_VALUE_HEADS, GROUP_QUERIES * HEAD_WIDTH), (QUERY_HEADS * HEAD_WIDTH // 128 + 1) ** -0.5, 2.0, ((0, 4), (1, 2))),
        "w_gate_up": bell_draw(splits[7], (MODEL_WIDTH, 2, FF), MODEL_WIDTH ** -0.5, 0.1875, ((0, 4), (2, 2))),
        "w_down": bell_draw(splits[8], (MODEL_WIDTH, FF), (FF // 4) ** -0.5, 0.21875, ((0, 4), (1, 2))),
        "cotangent": gaussian_with(splits[9], (TOKENS, MODEL_WIDTH), 1.0, 6.0, ((0, 16),), (0, 1, 16, 2.0)),
    }


@jax.custom_vjp
def lowered_input(v):
    return lax.optimization_barrier(v.astype(jnp.bfloat16)).astype(jnp.float32)

@jax.custom_vjp
def lowered_gradient(v):
    return v

def low_keep(v):
    return (lowered_input(v), None)

def low_pass(kept, grad):
    return (grad,)

def back_keep(v):
    return (v, None)

def back_low(kept, grad):
    return (lowered_input(grad),)
lowered_input.defvjp(low_keep, low_pass)
lowered_gradient.defvjp(back_keep, back_low)
epsilon = 1e-05
rope_base = 10000.0
masked_score = -1e+30
highest = lax.Precision.HIGHEST

def rms_scale(values, gain):
    return values * lax.rsqrt(lax.optimization_barrier(jnp.mean(values * values, axis=-1, keepdims=True)) + epsilon) * gain

def rope_tables(position):
    half_width = HEAD_WIDTH // 2
    frequency = jnp.power(rope_base, -2.0 * jnp.arange(half_width, dtype=jnp.float32) / HEAD_WIDTH)
    angles = position[:, None] * frequency[None, :]
    return (jnp.cos(angles), jnp.sin(angles))

def rotate_pairs(values, cosine_values, sine_values):
    half_width = values.shape[-1] // 2
    lower_half = values[..., :half_width]
    upper_half = values[..., half_width:]
    return jnp.concatenate([lower_half * cosine_values - upper_half * sine_values, upper_half * cosine_values + lower_half * sine_values], axis=-1)

def doc_begins(segment_index_row, start_row):
    matches = segment_index_row[:, None] == jnp.arange(start_row.shape[0], dtype=jnp.int32)[None, :]
    return lax.optimization_barrier(jnp.sum(jnp.where(matches, start_row[None, :], 0), axis=1)).astype(jnp.int32)

def sequence_layer(weight_set, layer_input, segment_index_row, start_row):
    gain_one, gain_two, qkv_weight, out_weight, gate_up_weight, down_weight = weight_set
    group_width = QUERY_HEADS // KEY_VALUE_HEADS
    query_feature_width = group_width * HEAD_WIDTH
    token_positions = jnp.arange(SEQUENCE_TOKENS, dtype=jnp.int32)
    begins = doc_begins(segment_index_row, start_row)
    cosine_values, sine_values = rope_tables((token_positions - begins).astype(jnp.float32))
    input_one = lowered_input(rms_scale(layer_input, gain_one))
    projected_rows = lowered_gradient(jnp.einsum('td,dhe->the', input_one, qkv_weight, precision=highest))
    query_matrix = lowered_input(rotate_pairs(projected_rows[..., :query_feature_width].reshape(SEQUENCE_TOKENS, KEY_VALUE_HEADS, group_width, HEAD_WIDTH), cosine_values[:, None, None, :], sine_values[:, None, None, :]))
    key_rows = lowered_input(rotate_pairs(projected_rows[..., query_feature_width:query_feature_width + HEAD_WIDTH], cosine_values[:, None, :], sine_values[:, None, :]))
    value_rows = lowered_input(projected_rows[..., query_feature_width + HEAD_WIDTH:])
    rows_per_block = min(512, SEQUENCE_TOKENS)
    block_list = SEQUENCE_TOKENS // rows_per_block
    score_scale = 1.0 / math.sqrt(HEAD_WIDTH)
    key_padding = segment_index_row < 0

    def attend_heads(packed):
        query_block, rows_block, segment_block, begin_block = packed
        scores = lowered_gradient(jnp.einsum('qhgd,khd->hgqk', query_block, key_rows, precision=highest) * score_scale)
        live_query = segment_block[:, None] >= 0
        causal = token_positions[None, :] <= rows_block[:, None]
        in_doc = token_positions[None, :] >= begin_block[:, None]
        allowed = causal & jnp.where(live_query, in_doc, key_padding[None, :])
        allowed = allowed | (token_positions[None, :] == rows_block[:, None])
        scores = jnp.where(allowed[None, None], scores, masked_score)
        probs = lowered_input(jax.nn.softmax(scores, axis=-1))
        return jnp.einsum('hgqk,khd->qhgd', probs, value_rows, precision=highest)
    attended_context = lax.map(jax.checkpoint(attend_heads), (query_matrix.reshape(block_list, rows_per_block, KEY_VALUE_HEADS, group_width, HEAD_WIDTH), token_positions.reshape(block_list, rows_per_block), segment_index_row.reshape(block_list, rows_per_block), begins.reshape(block_list, rows_per_block)))
    attended_context = lowered_input(lowered_gradient(attended_context.reshape(SEQUENCE_TOKENS, KEY_VALUE_HEADS, query_feature_width)))
    attention = lowered_gradient(jnp.einsum('the,dhe->td', attended_context, out_weight, precision=highest))
    residual = layer_input + attention
    input_two = lowered_input(rms_scale(residual, gain_two))
    gate_up = lowered_gradient(jnp.einsum('td,dcf->tcf', input_two, gate_up_weight, precision=highest))
    hidden = lowered_input(jax.nn.silu(gate_up[:, 0]) * gate_up[:, 1])
    feed = lowered_gradient(jnp.einsum('tf,df->td', hidden, down_weight, precision=highest))
    return residual + feed

def reference(tokens, segment_ids, doc_starts, norm1_gain, norm2_gain, query_key_value_weight, output_weight, w_gate_up, w_down, cotangent):
    seq_count = tokens.shape[0] // SEQUENCE_TOKENS
    weights = tuple((array_in.astype(jnp.float32) for array_in in (norm1_gain, norm2_gain, query_key_value_weight, output_weight, w_gate_up, w_down)))
    layer_input = tokens.astype(jnp.float32).reshape(seq_count, SEQUENCE_TOKENS, MODEL_WIDTH)
    segment_rows = segment_ids.reshape(seq_count, SEQUENCE_TOKENS)
    live_rows = (segment_ids >= 0).astype(jnp.float32)
    grad_out = (cotangent.astype(jnp.float32) * live_rows[:, None]).reshape(seq_count, SEQUENCE_TOKENS, MODEL_WIDTH)

    def forward(weight_set, inputs_all):

        def one_sequence(packed):
            return sequence_layer(weight_set, packed[0], packed[1], packed[2])
        return lax.map(jax.checkpoint(one_sequence), (inputs_all, segment_rows, doc_starts))
    layer_output, pullback = jax.vjp(forward, weights, layer_input)
    weight_grads, input_grad = pullback(grad_out)
    return (layer_output.reshape(TOKENS, MODEL_WIDTH).astype(jnp.bfloat16), input_grad.reshape(TOKENS, MODEL_WIDTH), weight_grads[0], weight_grads[1], weight_grads[2], weight_grads[3], weight_grads[4], weight_grads[5])
```

```python
import functools
import math

import jax
import jax.numpy as jnp
from jax import lax
from jax.experimental import pallas as pl
from jax.experimental.pallas import tpu as pltpu
from jax.sharding import PartitionSpec as P

QUERY_HEADS = 18
KEY_VALUE_HEADS = 6
HEAD_WIDTH = 64
GROUP = QUERY_HEADS // KEY_VALUE_HEADS
SEQ_CAP = 4096
DOC_FIRST = 2000

epsilon = 1e-05
rope_base = 10000.0
masked_score = -1e30
LOG2E = math.log2(math.e)
SCALE = 1.0 / math.sqrt(HEAD_WIDTH)
SCALE2 = SCALE * LOG2E
AXES = ("dp", "row", "col")
BF = jnp.bfloat16
F32 = jnp.float32


BQ = 512
BK = 256
TAIL = 64
LEAD = 256


def rms_parts(values):
    inverse = lax.rsqrt(jnp.mean(values * values, axis=-1, keepdims=True) + epsilon)
    return (values * inverse, inverse)


def rms_back(grad_normed, normed, inverse):
    return inverse * (grad_normed - normed * jnp.mean(grad_normed * normed, axis=-1, keepdims=True))


def rope_tables(position):
    half_width = HEAD_WIDTH // 2
    frequency = jnp.power(rope_base, -2.0 * jnp.arange(half_width, dtype=F32) / HEAD_WIDTH)
    angles = position[:, None] * frequency[None, :]
    return (jnp.cos(angles), jnp.sin(angles))


def rotate_pairs(values, cosine_values, sine_values):
    half_width = values.shape[-1] // 2
    lower_half = values[..., :half_width]
    upper_half = values[..., half_width:]
    return jnp.concatenate(
        [
            lower_half * cosine_values - upper_half * sine_values,
            upper_half * cosine_values + lower_half * sine_values,
        ],
        axis=-1,
    )


def dot(left, right, dims, out=F32):
    return lax.dot_general(left, right, (dims, ((), ())), preferred_element_type=out)


def attend_kernel(low_ref, q_ref, k_ref, v_ref, eb_ref, o_ref, lse_ref, m_s, acc_s, *, bq, bk, halo):
    i = pl.program_id(1)
    g = q_ref.shape[1]
    q = q_ref[0].reshape(g * bq, HEAD_WIDTH)
    m_s[...] = jnp.full(m_s.shape, masked_score, F32)
    acc_s[...] = jnp.zeros(acc_s.shape, F32)
    q_row = halo + i * bq + lax.broadcasted_iota(jnp.int32, (bq, bk), 0)
    begin = jnp.concatenate([eb_ref[...]] * (bk // 128), axis=1)
    col_id = lax.broadcasted_iota(jnp.int32, (bq, bk), 1)

    def body(j, carry):
        off = pl.multiple_of(j * bk, bk)
        k = k_ref[0, pl.ds(off, bk), :]
        v = v_ref[0, pl.ds(off, bk), :]
        s = dot(q, k, ((1,), (1,)))
        col = col_id + off
        ok = (col >= begin) & (col <= q_row)
        s = jnp.where(ok[None], s.reshape(g, bq, bk), masked_score).reshape(g * bq, bk)
        m0 = m_s[...]
        m1 = jnp.maximum(m0, jnp.max(s, axis=1, keepdims=True))
        p = jnp.exp2((s - jnp.concatenate([m1] * (bk // 128), axis=1)) * SCALE2).astype(BF)
        m_s[...] = m1
        acc_s[...] = acc_s[...] * jnp.exp2((m0 - m1) * SCALE2) + dot(p, v, ((1,), (0,)))
        return carry

    lax.fori_loop(low_ref[i], (halo + (i + 1) * bq) // bk, body, 0)
    acc = acc_s[...]
    total = acc[:, HEAD_WIDTH : HEAD_WIDTH + 1]
    o_ref[0] = (acc[:, :HEAD_WIDTH] / total).astype(o_ref.dtype).reshape(g, bq, HEAD_WIDTH)
    log_total = m_s[...] * SCALE2 + jnp.log(total) * LOG2E
    lse_ref[0, 0] = jnp.transpose(log_total)[0:1, :]


def attend(low, q, k, v, begin, *, bq, bk, halo):
    heads, g, rows, _ = q.shape
    keys = k.shape[1]
    blocks = rows // bq
    return pl.pallas_call(
        functools.partial(attend_kernel, bq=bq, bk=bk, halo=halo),
        out_shape=(
            jax.ShapeDtypeStruct((heads, g, rows, HEAD_WIDTH), BF),
            jax.ShapeDtypeStruct((heads, blocks, 1, g * bq), F32),
        ),
        grid_spec=pltpu.PrefetchScalarGridSpec(
            num_scalar_prefetch=1,
            grid=(heads, blocks),
            in_specs=[
                pl.BlockSpec((1, g, bq, HEAD_WIDTH), lambda h, i, low: (h, 0, i, 0)),
                pl.BlockSpec((1, keys, HEAD_WIDTH), lambda h, i, low: (h, 0, 0)),
                pl.BlockSpec((1, keys, 2 * HEAD_WIDTH), lambda h, i, low: (h, 0, 0)),
                pl.BlockSpec((bq, 128), lambda h, i, low: (i, 0)),
            ],
            out_specs=[
                pl.BlockSpec((1, g, bq, HEAD_WIDTH), lambda h, i, low: (h, 0, i, 0)),
                pl.BlockSpec((1, 1, 1, g * bq), lambda h, i, low: (h, i, 0, 0)),
            ],
            scratch_shapes=[pltpu.VMEM((g * bq, 128), F32), pltpu.VMEM((g * bq, 128), F32)],
        ),
        name="attend",
    )(low, q, k, v, begin)


def attend_back_kernel(
    low_ref, q_ref, k_ref, v_ref, do_ref, o_ref, lse_ref, eb_ref, dq_ref, dk_ref, dv_ref, dq_s, *, bq, bk, halo
):
    i = pl.program_id(1)
    g = q_ref.shape[1]

    @pl.when(i == 0)
    def _():
        dk_ref[...] = jnp.zeros(dk_ref.shape, F32)
        dv_ref[...] = jnp.zeros(dv_ref.shape, F32)

    q = q_ref[0].reshape(g * bq, HEAD_WIDTH)
    do = do_ref[0].reshape(g * bq, HEAD_WIDTH)
    o = o_ref[0].reshape(g * bq, HEAD_WIDTH)
    inner = jnp.sum(do.astype(F32) * o.astype(F32), axis=1, keepdims=True)
    inner_row = jnp.transpose(jnp.broadcast_to(inner, (g * bq, 128)))[0:1, :]
    lse_row = lse_ref[0, 0]
    dq_s[...] = jnp.zeros(dq_s.shape, F32)
    q_col = halo + i * bq + lax.broadcasted_iota(jnp.int32, (bk, bq), 1)
    row_id = lax.broadcasted_iota(jnp.int32, (bk, bq), 0)
    begin = eb_ref[...]

    def body(j, carry):
        off = pl.multiple_of(j * bk, bk)
        k = k_ref[0, pl.ds(off, bk), :]
        v = v_ref[0, pl.ds(off, bk), :]
        s = dot(k, q, ((1,), (1,)))
        row = row_id + off
        ok = (row >= begin) & (row <= q_col)
        p = jnp.where(jnp.concatenate([ok] * g, axis=1), jnp.exp2(s * SCALE2 - lse_row), 0.0)
        dv_ref[0, pl.ds(off, bk), :] += dot(p.astype(BF), do, ((1,), (0,)))
        dp = dot(v, do, ((1,), (1,)))
        ds = (p * (dp - inner_row)).astype(BF)
        dk_ref[0, pl.ds(off, bk), :] += dot(ds, q, ((1,), (0,)))
        dq_s[...] += dot(k, ds, ((0,), (0,)))
        return carry

    lax.fori_loop(low_ref[i], (halo + (i + 1) * bq) // bk, body, 0)
    dq_ref[0] = jnp.transpose(dq_s[...]).reshape(g, bq, HEAD_WIDTH) * SCALE

    @pl.when(i == pl.num_programs(1) - 1)
    def _():
        dk_ref[...] = dk_ref[...] * SCALE


def attend_back(low, q, k, v, do, o, lse, begin, *, bq, bk, halo):
    heads, g, rows, _ = q.shape
    keys = k.shape[1]
    blocks = rows // bq
    q_spec = pl.BlockSpec((1, g, bq, HEAD_WIDTH), lambda h, i, low: (h, 0, i, 0))
    k_spec = pl.BlockSpec((1, keys, HEAD_WIDTH), lambda h, i, low: (h, 0, 0))
    return pl.pallas_call(
        functools.partial(attend_back_kernel, bq=bq, bk=bk, halo=halo),
        out_shape=(
            jax.ShapeDtypeStruct((heads, g, rows, HEAD_WIDTH), F32),
            jax.ShapeDtypeStruct((heads, keys, HEAD_WIDTH), F32),
            jax.ShapeDtypeStruct((heads, keys, HEAD_WIDTH), F32),
        ),
        grid_spec=pltpu.PrefetchScalarGridSpec(
            num_scalar_prefetch=1,
            grid=(heads, blocks),
            in_specs=[
                q_spec,
                k_spec,
                k_spec,
                q_spec,
                q_spec,
                pl.BlockSpec((1, 1, 1, g * bq), lambda h, i, low: (h, i, 0, 0)),
                pl.BlockSpec((1, bq), lambda h, i, low: (0, i)),
            ],
            out_specs=[q_spec, k_spec, k_spec],
            scratch_shapes=[pltpu.VMEM((HEAD_WIDTH, g * bq), F32)],
        ),
        name="attend_back",
    )(low, q, k, v, do, o, lse, begin)


def make_local(n_dp, n_row, n_col):
    assert n_row == 2 and n_dp % 4 == 0

    def lin(d, r, z):
        return (d * n_row + r) * n_col + z

    def perm_of(target):
        pairs = []
        for d in range(n_dp):
            for r in range(n_row):
                for z in range(n_col):
                    to = target(d, r, z)
                    if to is not None:
                        pairs.append((lin(d, r, z), lin(*to)))
        return pairs

    def mover(target):
        pairs = perm_of(target)
        return lambda value: lax.ppermute(value, AXES, pairs)

    to_core = mover(lambda d, r, z: (d ^ 1, r, z))
    to_x = mover(lambda d, r, z: (d, 1 - r, z))
    to_y = mover(lambda d, r, z: (d ^ 2, r, z))
    diag_to_core = mover(lambda d, r, z: (d ^ 1, r, z) if d % 2 == r else None)
    diag_to_x = mover(lambda d, r, z: (d, 1 - r, z) if d % 2 == r else None)
    off_to_x = mover(lambda d, r, z: (d, 1 - r, z) if d % 2 != r else None)
    to_z = [mover(lambda d, r, z, s=s: (d, r, (z + s) % n_col)) for s in range(n_col)]
    to_group = [mover(lambda d, r, z, s=s: ((d + 4 * s) % n_dp, r, z)) for s in range(n_dp // 4)]

    def local(
        tokens,
        segment_ids,
        doc_starts,
        norm1_gain,
        norm2_gain,
        query_key_value_weight,
        output_weight,
        w_gate_up,
        w_down,
        cotangent,
    ):
        tok_count, width = tokens.shape
        dpi = lax.axis_index("dp")
        row = lax.axis_index("row")
        column = lax.axis_index("col")
        core = dpi % 2
        ybit = (dpi // 2) % 2
        diag = core == row
        heads = query_key_value_weight.shape[1]
        q_width = GROUP * HEAD_WIDTH
        seq_len = min(SEQ_CAP, tok_count * n_col)
        per_seq = seq_len // tok_count
        shard = column % per_seq
        seq_index = column // per_seq
        halo = LEAD + tok_count
        halo_to = {
            1: mover(lambda d, r, z: (d, r, z + 1) if z % per_seq + 1 < per_seq else None),
            2: mover(lambda d, r, z: (d, r, z + 2) if z % per_seq == 1 else None),
        }
        halo_back = {
            1: mover(lambda d, r, z: (d, r, z - 1) if z % per_seq >= 1 else None),
            2: mover(lambda d, r, z: (d, r, z - 2) if z % per_seq == 3 else None),
        }

        def two(own, other, bit, axis):
            first = jnp.where(bit == 0, own, other)
            second = jnp.where(bit == 0, other, own)
            return jnp.stack([first, second], axis=axis)

        def gather_weight(shard_rows, order):
            rows, features = shard_rows.shape
            part = rows // 4
            quarters = shard_rows.reshape(4, part, features)
            mine = lax.dynamic_index_in_dim(quarters, 2 * ybit + row, 0, keepdims=False)
            sent = lax.dynamic_index_in_dim(quarters, 2 * ybit + 1 - row, 0, keepdims=False)
            piece = jnp.where(diag, mine, diag_to_x(sent))
            stacked = jnp.zeros((n_col, part, features), BF)
            stacked = lax.dynamic_update_index_in_dim(stacked, piece, column, 0)
            for step in range(1, n_col):
                stacked = lax.dynamic_update_index_in_dim(
                    stacked, to_z[step](piece), (column - step) % n_col, 0
                )
            if order == "xy":
                pair = two(stacked, to_x(stacked), row, 1)
                full = two(pair, to_y(pair), ybit, 1)
            else:
                pair = two(stacked, to_y(stacked), ybit, 1)
                full = two(pair, to_x(pair), row, 2)
            return full.reshape(n_col * rows, features)

        def reduce_weight(partial, order):
            total_rows, features = partial.shape
            part = total_rows // (4 * n_col)
            value = partial.reshape(n_col, 2, 2, part, features)

            def halve(array, bit, axis, move):
                kept = lax.dynamic_index_in_dim(array, bit, axis, keepdims=False)
                sent = lax.dynamic_index_in_dim(array, 1 - bit, axis, keepdims=False)
                return (kept.astype(F32) + move(sent).astype(F32)).astype(BF)

            if order == "xy":
                value = halve(value, row, 2, to_x)
                value = halve(value, ybit, 1, to_y)
            else:
                value = halve(value, ybit, 1, to_y)
                value = halve(value, row, 1, to_x)
            acc = lax.dynamic_index_in_dim(value, column, 0, keepdims=False).astype(F32)
            for step in range(1, n_col):
                acc = acc + to_z[step](
                    lax.dynamic_index_in_dim(value, (column + step) % n_col, 0, keepdims=False)
                ).astype(F32)
            piece = acc.astype(BF)
            if n_dp > 4:
                groups = n_dp // 4
                mine = dpi // 4
                stacked = jnp.zeros((groups,) + piece.shape, BF)
                stacked = lax.dynamic_update_index_in_dim(stacked, piece, mine, 0)
                for step in range(1, groups):
                    stacked = lax.dynamic_update_index_in_dim(
                        stacked, to_group[step](piece), (mine - step) % groups, 0
                    )
                piece = jnp.sum(stacked.astype(F32), axis=0).astype(BF)
            pair = two(piece, off_to_x(piece), row, 0)
            full = two(pair, to_y(pair), ybit, 0).reshape(4 * part, features)
            return jnp.where(diag, full, diag_to_core(full)).astype(F32)

        def same_chip(value):
            return jnp.where(diag, value, diag_to_core(value))

        tokens_here = same_chip(tokens)
        whole_numbers = same_chip(jnp.concatenate([segment_ids, doc_starts.reshape(-1)]))
        cotangent_here = same_chip(cotangent)
        segment_here = whole_numbers[:tok_count]
        starts_here = whole_numbers[tok_count:].reshape(doc_starts.shape)

        gains = jnp.stack([norm1_gain, norm2_gain])
        gain_rows = jnp.zeros((n_col,) + gains.shape, BF)
        gain_rows = lax.dynamic_update_index_in_dim(gain_rows, gains, column, 0)
        for step in range(1, n_col):
            gain_rows = lax.dynamic_update_index_in_dim(
                gain_rows, to_z[step](gains), (column - step) % n_col, 0
            )
        gain_all = jnp.moveaxis(gain_rows, 1, 0).reshape(2, width).astype(F32)
        gain_one, gain_two = gain_all[0], gain_all[1]

        shard_rows = query_key_value_weight.shape[0]
        qkv_shard = jnp.concatenate(
            [
                query_key_value_weight[:, :, :q_width].reshape(shard_rows, heads * q_width),
                query_key_value_weight[:, :, q_width : q_width + HEAD_WIDTH].reshape(shard_rows, -1),
                query_key_value_weight[:, :, q_width + HEAD_WIDTH :].reshape(shard_rows, -1),
            ],
            axis=1,
        )
        full_qkv = gather_weight(qkv_shard, "xy")
        full_out = gather_weight(output_weight.reshape(shard_rows, -1), "yx")
        full_gate_up = gather_weight(w_gate_up.reshape(shard_rows, -1), "xy")
        full_down = gather_weight(w_down, "yx")
        hidden_width = w_down.shape[1]

        chosen = jnp.arange(doc_starts.shape[0], dtype=jnp.int32) == seq_index
        start_row = jnp.sum(jnp.where(chosen[:, None], starts_here, 0), axis=0)
        matches = segment_here[:, None] == jnp.arange(doc_starts.shape[1], dtype=jnp.int32)[None, :]
        begins = jnp.sum(jnp.where(matches, start_row[None, :], 0), axis=1)
        in_seq = shard * tok_count + jnp.arange(tok_count, dtype=jnp.int32)
        live = segment_here >= 0
        lived = jnp.sum(live.astype(jnp.int32)).reshape(1)
        lived_one = halo_to[1](lived)[0]
        lived_two = halo_to[2](lived)[0]
        lived = lived[0]
        pad_from = jnp.where(
            lived > 0,
            shard * tok_count + lived,
            jnp.where(
                lived_one > 0,
                (shard - 1) * tok_count + lived_one,
                (shard - 2) * tok_count + lived_two,
            ),
        )
        base = shard * tok_count - halo
        begin_key = jnp.where(live, begins, pad_from) - base
        low = begin_key[::BQ] // BK
        begin_wide = jnp.broadcast_to(begin_key[:, None], (tok_count, 128))
        cosine_values, sine_values = rope_tables((in_seq - begins).astype(F32))

        layer_input = tokens_here.astype(F32)
        normed_one, inverse_one = rms_parts(layer_input)
        input_one = (normed_one * gain_one).astype(BF)
        projected = dot(input_one, full_qkv, ((1,), (0,)))
        all_q = heads * q_width
        all_k = heads * HEAD_WIDTH
        queries = rotate_pairs(
            projected[:, :all_q].reshape(tok_count, heads * GROUP, HEAD_WIDTH),
            cosine_values[:, None, :],
            sine_values[:, None, :],
        ).astype(BF)
        keys = rotate_pairs(
            projected[:, all_q : all_q + all_k].reshape(tok_count, heads, HEAD_WIDTH),
            cosine_values[:, None, :],
            sine_values[:, None, :],
        ).astype(BF)
        key_values = jnp.concatenate(
            [keys.reshape(tok_count, all_k), projected[:, all_q + all_k :].astype(BF)], axis=1
        )
        kv_all = jnp.concatenate(
            [
                jnp.zeros((LEAD - TAIL, 2 * all_k), BF),
                halo_to[2](key_values[tok_count - TAIL :]),
                halo_to[1](key_values),
                key_values,
            ],
            axis=0,
        )
        kv_heads = jnp.moveaxis(kv_all.reshape(halo + tok_count, 2 * heads, HEAD_WIDTH), 1, 0)
        k_heads = kv_heads[:heads]
        v_heads = kv_heads[heads:]
        v_wide = jnp.concatenate([v_heads, jnp.ones(v_heads.shape, BF)], axis=-1)
        q_heads = jnp.moveaxis(queries, 1, 0).reshape(heads, GROUP, tok_count, HEAD_WIDTH)
        context_heads, log_totals = attend(
            low, q_heads, k_heads, v_wide, begin_wide, bq=BQ, bk=BK, halo=halo
        )
        context = jnp.moveaxis(context_heads.reshape(heads * GROUP, tok_count, HEAD_WIDTH), 0, 1).reshape(
            tok_count, all_q
        )
        attention = dot(context, full_out, ((1,), (1,)))
        residual = layer_input + attention + to_core(attention.astype(BF)).astype(F32)
        normed_two, inverse_two = rms_parts(residual)
        input_two = (normed_two * gain_two).astype(BF)
        gate_up = dot(input_two, full_gate_up, ((1,), (0,)))
        gate_value = gate_up[:, :hidden_width]
        up_value = gate_up[:, hidden_width:]
        sigmoid_gate = jax.nn.sigmoid(gate_value)
        gate_act = gate_value * sigmoid_gate
        hidden = (gate_act * up_value).astype(BF)
        feed = dot(hidden, full_down, ((1,), (1,)))
        output_here = (residual + feed + to_core(feed.astype(BF)).astype(F32)).astype(BF)
        layer_output = jnp.where(diag, output_here, diag_to_x(output_here))

        grad_out = cotangent_here.astype(F32) * live.astype(F32)[:, None]
        grad_feed = grad_out.astype(BF)
        grad_hidden = dot(grad_feed, full_down, ((1,), (0,)))
        grad_gate = grad_hidden * up_value * sigmoid_gate * (1.0 + gate_value * (1.0 - sigmoid_gate))
        grad_up = grad_hidden * gate_act
        grad_gate_up = jnp.concatenate([grad_gate, grad_up], axis=1).astype(BF)
        part_two = dot(grad_gate_up, full_gate_up, ((1,), (1,)))
        down_grad = reduce_weight(dot(grad_feed, hidden, ((0,), (0,)), BF), "yx")
        gate_up_grad = reduce_weight(dot(input_two, grad_gate_up, ((0,), (0,)), BF), "xy")
        grad_input_two = part_two + to_core(part_two.astype(BF)).astype(F32)
        gain_two_grad = jnp.sum(grad_input_two * normed_two, axis=0)
        grad_residual = grad_out + rms_back(grad_input_two * gain_two, normed_two, inverse_two)
        grad_attention = grad_residual.astype(BF)
        out_grad = reduce_weight(dot(grad_attention, context, ((0,), (0,)), BF), "yx")
        grad_context = dot(grad_attention, full_out, ((1,), (0,))).astype(BF)
        grad_heads = jnp.moveaxis(grad_context.reshape(tok_count, heads * GROUP, HEAD_WIDTH), 1, 0).reshape(
            heads, GROUP, tok_count, HEAD_WIDTH
        )
        dq, dk, dv = attend_back(
            low,
            q_heads,
            k_heads,
            v_heads,
            grad_heads,
            context_heads,
            log_totals,
            begin_key[None, :],
            bq=BQ,
            bk=BK,
            halo=halo,
        )
        dkv = jnp.moveaxis(jnp.concatenate([dk, dv], axis=0), 0, 1).reshape(halo + tok_count, 2 * all_k)
        near = halo_back[1](dkv[LEAD:halo].astype(BF)).astype(F32)
        far = halo_back[2](dkv[LEAD - TAIL : LEAD].astype(BF)).astype(F32)
        own = dkv[halo:] + near
        own = jnp.concatenate([own[: tok_count - TAIL], own[tok_count - TAIL :] + far], axis=0)
        query_back = rotate_pairs(
            jnp.moveaxis(dq.reshape(heads * GROUP, tok_count, HEAD_WIDTH), 0, 1),
            cosine_values[:, None, :],
            -sine_values[:, None, :],
        ).reshape(tok_count, all_q)
        key_back = rotate_pairs(
            own[:, :all_k].reshape(tok_count, heads, HEAD_WIDTH),
            cosine_values[:, None, :],
            -sine_values[:, None, :],
        ).reshape(tok_count, all_k)
        grad_projected = jnp.concatenate([query_back, key_back, own[:, all_k:]], axis=1).astype(BF)
        part_one = dot(grad_projected, full_qkv, ((1,), (1,)))
        grad_input_one = part_one + to_core(part_one.astype(BF)).astype(F32)
        gain_one_grad = jnp.sum(grad_input_one * normed_one, axis=0)
        input_here = (
            grad_residual + rms_back(grad_input_one * gain_one, normed_one, inverse_one)
        ).astype(BF)
        input_grad = jnp.where(diag, input_here, diag_to_x(input_here)).astype(F32)
        qkv_partial = dot(input_one, grad_projected, ((0,), (0,)), BF)
        qkv_sum = reduce_weight(
            jnp.concatenate(
                [qkv_partial, gain_one_grad.astype(BF)[:, None], gain_two_grad.astype(BF)[:, None]], axis=1
            ),
            "xy",
        )
        features = qkv_partial.shape[1]
        qkv_grad = jnp.concatenate(
            [
                qkv_sum[:, :all_q].reshape(shard_rows, heads, q_width),
                qkv_sum[:, all_q : all_q + all_k].reshape(shard_rows, heads, HEAD_WIDTH),
                qkv_sum[:, all_q + all_k : features].reshape(shard_rows, heads, HEAD_WIDTH),
            ],
            axis=2,
        )
        gain_sums = jnp.transpose(qkv_sum[:, features:])
        gain_other = to_x(gain_sums.astype(BF)).astype(F32)
        gain_sums = jnp.where(row == 0, gain_sums, gain_other)
        return (
            layer_output,
            input_grad,
            gain_sums[0],
            gain_sums[1],
            qkv_grad,
            out_grad.reshape(output_weight.shape),
            gate_up_grad.reshape(w_gate_up.shape),
            down_grad,
        )

    return local


def solution(mesh):
    placed = (
        P(("dp", "col"), None),
        P(("dp", "col")),
        P("dp", None),
        P("col"),
        P("col"),
        P("col", "row", None),
        P("col", "row", None),
        P("col", None, "row"),
        P("col", "row"),
        P(("dp", "col"), None),
    )
    return jax.shard_map(
        make_local(mesh.shape["dp"], mesh.shape["row"], mesh.shape["col"]),
        mesh=mesh,
        in_specs=placed,
        out_specs=(
            P(("dp", "col"), None),
            P(("dp", "col"), None),
            P("col"),
            P("col"),
            P("col", "row", None),
            P("col", "row", None),
            P("col", None, "row"),
            P("col", "row"),
        ),
        check_vma=False,
    )
```

```python
import functools
import math

import jax
import jax.numpy as jnp
from jax import lax
from jax.experimental import pallas as pl
from jax.experimental.pallas import tpu as pltpu
from jax.sharding import PartitionSpec as P

QUERY_HEADS = 18
KEY_VALUE_HEADS = 6
HEAD_WIDTH = 64
GROUP = QUERY_HEADS // KEY_VALUE_HEADS
SEQ_CAP = 4096
DOC_FIRST = 2000

epsilon = 1e-05
rope_base = 10000.0
masked_score = -1e30
LOG2E = math.log2(math.e)
SCALE = 1.0 / math.sqrt(HEAD_WIDTH)
SCALE2 = SCALE * LOG2E
AXES = ("dp", "row", "col")
BF = jnp.bfloat16
F32 = jnp.float32


BQ = 512
BK = 256
TAIL = 64
LEAD = 256


def rms_parts(values):
    inverse = lax.rsqrt(jnp.mean(values * values, axis=-1, keepdims=True) + epsilon)
    return (values * inverse, inverse)


def rms_back(grad_normed, normed, inverse):
    return inverse * (grad_normed - normed * jnp.mean(grad_normed * normed, axis=-1, keepdims=True))


def rope_tables(position):
    half_width = HEAD_WIDTH // 2
    frequency = jnp.power(rope_base, -2.0 * jnp.arange(half_width, dtype=F32) / HEAD_WIDTH)
    angles = position[:, None] * frequency[None, :]
    return (jnp.cos(angles), jnp.sin(angles))


def dot(left, right, dims, out=F32):
    return lax.dot_general(left, right, (dims, ((), ())), preferred_element_type=out)


def swap_halves(values):
    lane = lax.broadcasted_iota(jnp.int32, values.shape, 1)
    up = pltpu.roll(values, 96, 1)
    down = pltpu.roll(values, 32, 1)
    return jnp.where(lane % HEAD_WIDTH < HEAD_WIDTH // 2, up, down)


def project_kernel(x_ref, gain_ref, w_ref, cq_ref, sq_ref, ck_ref, sk_ref, in_ref, q_ref, kv_ref):
    x = x_ref[...].astype(F32)
    inverse = lax.rsqrt(jnp.mean(x * x, axis=-1, keepdims=True) + epsilon)
    scaled = (x * inverse * gain_ref[...]).astype(BF)
    in_ref[...] = scaled
    heads = kv_ref.shape[1] // 128
    for chunk in range(w_ref.shape[1] // 128):
        u = dot(scaled, w_ref[:, 128 * chunk : 128 * chunk + 128], ((1,), (0,)))
        if chunk < heads:
            turned = u * ck_ref[...] + swap_halves(u) * sk_ref[...]
            kv_ref[:, 128 * chunk : 128 * chunk + 128] = turned.astype(BF)
        else:
            turned = (u * cq_ref[...] + swap_halves(u) * sq_ref[...]).astype(BF)
            first = 2 * (chunk - heads)
            q_ref[first] = turned[:, :HEAD_WIDTH]
            if first + 1 < q_ref.shape[0]:
                q_ref[first + 1] = turned[:, HEAD_WIDTH:]


def project(x, gain, w, tables, q_heads, kv_heads):
    rows, width = x.shape
    block = min(256, rows)
    row_spec = lambda n: pl.BlockSpec((block, n), lambda i: (i, 0))
    table = row_spec(128)
    return pl.pallas_call(
        project_kernel,
        grid=(rows // block,),
        out_shape=(
            jax.ShapeDtypeStruct((rows, width), BF),
            jax.ShapeDtypeStruct((q_heads, rows, HEAD_WIDTH), BF),
            jax.ShapeDtypeStruct((rows, kv_heads * 128), BF),
        ),
        in_specs=[
            row_spec(width),
            pl.BlockSpec((1, width), lambda i: (0, 0)),
            pl.BlockSpec(w.shape, lambda i: (0, 0)),
            table,
            table,
            table,
            table,
        ],
        out_specs=[
            row_spec(width),
            pl.BlockSpec((q_heads, block, HEAD_WIDTH), lambda i: (0, i, 0)),
            row_spec(kv_heads * 128),
        ],
        name="project",
    )(x, gain, w, *tables)


def stage_keys(k_s, v_s, own, near, far, lead, tail, lanes):
    n = near.shape[0]
    k_s[: lead - tail] = jnp.zeros((lead - tail, k_s.shape[1]), BF)
    v_s[: lead - tail] = jnp.zeros((lead - tail, v_s.shape[1]), BF)
    for first, ref in ((lead - tail, far), (lead, near), (lead + n, own)):
        rows = ref.shape[0]
        pair = ref[:, lanes : lanes + 128]
        k_s[first : first + rows] = pair[:, :HEAD_WIDTH]
        values = pair[:, HEAD_WIDTH:]
        if v_s.shape[1] == 128:
            values = jnp.concatenate([values, jnp.ones(values.shape, BF)], axis=1)
        v_s[first : first + rows] = values


def attend_kernel(
    low_ref, q_ref, own_ref, near_ref, far_ref, eb_ref, o_ref, lse_ref, k_s, v_s, m_s, acc_s, *, bq, bk, lead, tail
):
    i = pl.program_id(0)
    h = pl.program_id(1)
    heads = k_s.shape[0]
    g = q_ref.shape[0]
    halo = lead + near_ref.shape[0]

    @pl.when((i == 0) & (h == 0))
    def _():
        for head in range(heads):
            stage_keys(k_s.at[head], v_s.at[head], own_ref, near_ref, far_ref, lead, tail, 128 * head)

    q = q_ref[...].reshape(g * bq, HEAD_WIDTH)
    m_s[...] = jnp.full(m_s.shape, masked_score, F32)
    acc_s[...] = jnp.zeros(acc_s.shape, F32)
    q_row = halo + i * bq + lax.broadcasted_iota(jnp.int32, (bq, bk), 0)
    begin = jnp.concatenate([eb_ref[...]] * (bk // 128), axis=1)
    col_id = lax.broadcasted_iota(jnp.int32, (bq, bk), 1)

    def body(j, carry):
        off = pl.multiple_of(j * bk, bk)
        k = k_s[h, pl.ds(off, bk), :]
        v = v_s[h, pl.ds(off, bk), :]
        s = dot(q, k, ((1,), (1,)))
        col = col_id + off
        ok = (col >= begin) & (col <= q_row)
        s = jnp.where(ok[None], s.reshape(g, bq, bk), masked_score).reshape(g * bq, bk)
        m0 = m_s[...]
        m1 = jnp.maximum(m0, jnp.max(s, axis=1, keepdims=True))
        p = jnp.exp2((s - jnp.concatenate([m1] * (bk // 128), axis=1)) * SCALE2).astype(BF)
        m_s[...] = m1
        acc_s[...] = acc_s[...] * jnp.exp2((m0 - m1) * SCALE2) + dot(p, v, ((1,), (0,)))
        return carry

    lax.fori_loop(low_ref[i], (halo + (i + 1) * bq) // bk, body, 0)
    acc = acc_s[...]
    total = acc[:, HEAD_WIDTH : HEAD_WIDTH + 1]
    part = (acc[:, :HEAD_WIDTH] / total).astype(BF).reshape(g, bq, HEAD_WIDTH)
    packed = jnp.concatenate([part[n] for n in range(g)], axis=1)
    for head in range(heads):

        @pl.when(h == head)
        def _():
            o_ref[:, head * g * HEAD_WIDTH : (head + 1) * g * HEAD_WIDTH] = packed

    log_total = m_s[...] * SCALE2 + jnp.log(total) * LOG2E
    lse_ref[0, 0] = jnp.transpose(log_total)[0:1, :]


def attend(low, q, own, near, far, begin, *, heads, bq, bk, lead, tail):
    g = q.shape[0] // heads
    rows = q.shape[1]
    keys = lead + near.shape[0] + own.shape[0]
    blocks = rows // bq
    whole = lambda array: pl.BlockSpec(array.shape, lambda i, h, low: (0, 0))
    return pl.pallas_call(
        functools.partial(attend_kernel, bq=bq, bk=bk, lead=lead, tail=tail),
        out_shape=(
            jax.ShapeDtypeStruct((rows, heads * g * HEAD_WIDTH), BF),
            jax.ShapeDtypeStruct((heads, blocks, 1, g * bq), F32),
        ),
        grid_spec=pltpu.PrefetchScalarGridSpec(
            num_scalar_prefetch=1,
            grid=(blocks, heads),
            in_specs=[
                pl.BlockSpec((g, bq, HEAD_WIDTH), lambda i, h, low: (h, i, 0)),
                whole(own),
                whole(near),
                whole(far),
                pl.BlockSpec((bq, 128), lambda i, h, low: (i, 0)),
            ],
            out_specs=[
                pl.BlockSpec((bq, heads * g * HEAD_WIDTH), lambda i, h, low: (i, 0)),
                pl.BlockSpec((1, 1, 1, g * bq), lambda i, h, low: (h, i, 0, 0)),
            ],
            scratch_shapes=[
                pltpu.VMEM((heads, keys, HEAD_WIDTH), BF),
                pltpu.VMEM((heads, keys, 128), BF),
                pltpu.VMEM((g * bq, 128), F32),
                pltpu.VMEM((g * bq, 128), F32),
            ],
        ),
        name="attend",
    )(low, q, own, near, far, begin)


def attend_back_kernel(
    low_ref,
    q_ref,
    own_ref,
    near_ref,
    far_ref,
    do_ref,
    o_ref,
    lse_ref,
    eb_ref,
    cos_ref,
    sin_ref,
    dq_ref,
    d_own_ref,
    d_near_ref,
    d_far_ref,
    k_s,
    v_s,
    dk_s,
    dv_s,
    dq_s,
    *,
    head,
    bq,
    bk,
    lead,
    tail,
):
    i = pl.program_id(0)
    g = q_ref.shape[0]
    near_rows = near_ref.shape[0]
    halo = lead + near_rows

    @pl.when(i == 0)
    def _():
        stage_keys(k_s, v_s, own_ref, near_ref, far_ref, lead, tail, 128 * head)
        dk_s[...] = jnp.zeros(dk_s.shape, F32)
        dv_s[...] = jnp.zeros(dv_s.shape, F32)

    def rows_of(ref):
        first = head * g * HEAD_WIDTH
        return jnp.concatenate(
            [ref[:, first + n * HEAD_WIDTH : first + (n + 1) * HEAD_WIDTH] for n in range(g)], axis=0
        )

    q = q_ref[...].reshape(g * bq, HEAD_WIDTH)
    do = rows_of(do_ref)
    inner = jnp.sum(do.astype(F32) * rows_of(o_ref).astype(F32), axis=1, keepdims=True)
    inner_row = jnp.transpose(jnp.broadcast_to(inner, (g * bq, 128)))[0:1, :]
    lse_row = lse_ref[0, 0]
    dq_s[...] = jnp.zeros(dq_s.shape, F32)
    q_col = halo + i * bq + lax.broadcasted_iota(jnp.int32, (bk, bq), 1)
    row_id = lax.broadcasted_iota(jnp.int32, (bk, bq), 0)
    begin = eb_ref[...]

    def body(j, carry):
        off = pl.multiple_of(j * bk, bk)
        k = k_s[pl.ds(off, bk), :]
        v = v_s[pl.ds(off, bk), :]
        s = dot(k, q, ((1,), (1,)))
        row = row_id + off
        ok = (row >= begin) & (row <= q_col)
        p = jnp.where(jnp.concatenate([ok] * g, axis=1), jnp.exp2(s * SCALE2 - lse_row), 0.0)
        dv_s[pl.ds(off, bk), :] += dot(p.astype(BF), do, ((1,), (0,)))
        dp = dot(v, do, ((1,), (1,)))
        ds = (p * (dp - inner_row)).astype(BF)
        dk_s[pl.ds(off, bk), :] += dot(ds, q, ((1,), (0,)))
        dq_s[...] += dot(k, ds, ((0,), (0,)))
        return carry

    lax.fori_loop(low_ref[i], (halo + (i + 1) * bq) // bk, body, 0)
    half = HEAD_WIDTH // 2
    parts = []
    for n in range(g):
        u = dq_s[:, n * bq : (n + 1) * bq] * SCALE
        turned = u * cos_ref[...] - jnp.concatenate([u[half:], u[:half]], axis=0) * sin_ref[...]
        parts.append(jnp.transpose(turned).astype(BF))
    dq_ref[...] = jnp.concatenate(parts, axis=1)

    @pl.when(i == pl.num_programs(0) - 1)
    def _():
        both = lambda first, rows: jnp.concatenate(
            [dk_s[first : first + rows] * SCALE, dv_s[first : first + rows]], axis=1
        )
        d_far_ref[...] = both(lead - tail, tail).astype(BF)
        d_near_ref[...] = both(lead, near_rows).astype(BF)
        d_own_ref[...] = both(halo, d_own_ref.shape[0])


def attend_back(low, q, own, near, far, do, o, lse, begin, cos_t, sin_t, *, head, heads, bq, bk, lead, tail):
    g = q.shape[0] // heads
    rows = q.shape[1]
    keys = lead + near.shape[0] + own.shape[0]
    blocks = rows // bq
    whole = lambda shape: pl.BlockSpec(shape, lambda i, low: (0, 0))
    packed = pl.BlockSpec((bq, do.shape[1]), lambda i, low: (i, 0))
    table = pl.BlockSpec((HEAD_WIDTH, bq), lambda i, low: (0, i))
    return pl.pallas_call(
        functools.partial(attend_back_kernel, head=head, bq=bq, bk=bk, lead=lead, tail=tail),
        out_shape=(
            jax.ShapeDtypeStruct((rows, g * HEAD_WIDTH), BF),
            jax.ShapeDtypeStruct((own.shape[0], 128), F32),
            jax.ShapeDtypeStruct((near.shape[0], 128), BF),
            jax.ShapeDtypeStruct((tail, 128), BF),
        ),
        grid_spec=pltpu.PrefetchScalarGridSpec(
            num_scalar_prefetch=1,
            grid=(blocks,),
            in_specs=[
                pl.BlockSpec((g, bq, HEAD_WIDTH), lambda i, low: (head, i, 0)),
                whole(own.shape),
                whole(near.shape),
                whole(far.shape),
                packed,
                packed,
                pl.BlockSpec((1, 1, 1, g * bq), lambda i, low: (head, i, 0, 0)),
                pl.BlockSpec((1, bq), lambda i, low: (0, i)),
                table,
                table,
            ],
            out_specs=[
                pl.BlockSpec((bq, g * HEAD_WIDTH), lambda i, low: (i, 0)),
                whole((own.shape[0], 128)),
                whole((near.shape[0], 128)),
                whole((tail, 128)),
            ],
            scratch_shapes=[
                pltpu.VMEM((keys, HEAD_WIDTH), BF),
                pltpu.VMEM((keys, HEAD_WIDTH), BF),
                pltpu.VMEM((keys, HEAD_WIDTH), F32),
                pltpu.VMEM((keys, HEAD_WIDTH), F32),
                pltpu.VMEM((HEAD_WIDTH, g * bq), F32),
            ],
        ),
        name="attend_back",
    )(low, q, own, near, far, do, o, lse, begin, cos_t, sin_t)


def unproject_kernel(*refs, heads):
    q_refs, own_refs, near_refs = refs[:heads], refs[heads : 2 * heads], refs[2 * heads : 3 * heads]
    far_ref, ck_ref, sk_ref, w_ref, gp_ref, part_ref, low_ref = refs[3 * heads :]
    rows = gp_ref.shape[0]
    tail = far_ref.shape[0]
    last = (pl.program_id(0) == pl.num_programs(0) - 1).astype(F32)
    for h in range(heads):
        x = own_refs[h][...] + near_refs[h][...].astype(F32)
        far = far_ref[:, 128 * h : 128 * h + 128].astype(F32) * last
        x = jnp.concatenate([x[: rows - tail], x[rows - tail :] + far], axis=0)
        turned = x * ck_ref[...] - swap_halves(x) * sk_ref[...]
        gp_ref[:, 128 * h : 128 * h + 128] = turned.astype(BF)
    pieces = [ref[...] for ref in q_refs]
    used = sum(piece.shape[1] for piece in pieces)
    spare = gp_ref.shape[1] - 128 * heads - used
    pieces.append(jnp.zeros((rows, spare), BF))
    gp_ref[:, 128 * heads :] = jnp.concatenate(pieces, axis=1)
    part = dot(gp_ref[...], w_ref[...], ((1,), (1,)))
    part_ref[...] = part
    low_ref[...] = part.astype(BF)


def unproject(q_parts, own_parts, near_parts, far, ck, sk, w):
    heads = len(q_parts)
    rows = own_parts[0].shape[0]
    width, features = w.shape
    block = min(256, rows)
    row_spec = lambda n: pl.BlockSpec((block, n), lambda i: (i, 0))
    return pl.pallas_call(
        functools.partial(unproject_kernel, heads=heads),
        grid=(rows // block,),
        out_shape=(
            jax.ShapeDtypeStruct((rows, features), BF),
            jax.ShapeDtypeStruct((rows, width), F32),
            jax.ShapeDtypeStruct((rows, width), BF),
        ),
        in_specs=[row_spec(part.shape[1]) for part in q_parts]
        + [row_spec(128)] * (2 * heads)
        + [
            pl.BlockSpec(far.shape, lambda i: (0, 0)),
            row_spec(128),
            row_spec(128),
            pl.BlockSpec(w.shape, lambda i: (0, 0)),
        ],
        out_specs=[row_spec(features), row_spec(width), row_spec(width)],
        name="unproject",
    )(*q_parts, *own_parts, *near_parts, far, ck, sk, w)


def make_local(n_dp, n_row, n_col):
    assert n_row == 2 and n_dp % 4 == 0

    def lin(d, r, z):
        return (d * n_row + r) * n_col + z

    def mover(target):
        pairs = []
        for d in range(n_dp):
            for r in range(n_row):
                for z in range(n_col):
                    to = target(d, r, z)
                    if to is not None:
                        pairs.append((lin(d, r, z), lin(*to)))
        return lambda value: lax.ppermute(value, AXES, pairs)

    to_core = mover(lambda d, r, z: (d ^ 1, r, z))
    to_x = mover(lambda d, r, z: (d, 1 - r, z))
    to_y = mover(lambda d, r, z: (d ^ 2, r, z))
    diag_to_core = mover(lambda d, r, z: (d ^ 1, r, z) if d % 2 == r else None)
    diag_to_x = mover(lambda d, r, z: (d, 1 - r, z) if d % 2 == r else None)
    off_to_x = mover(lambda d, r, z: (d, 1 - r, z) if d % 2 != r else None)
    even_to_core = mover(lambda d, r, z: (d ^ 1, r, z) if d % 2 == 0 else None)
    to_z = [mover(lambda d, r, z, s=s: (d, r, (z + s) % n_col)) for s in range(n_col)]
    col_bits = [mover(lambda d, r, z, b=b: (d, r, z ^ b)) for b in (1, 2, 4, 8, 16, 32) if b < n_col]
    dp_bits = [mover(lambda d, r, z, b=b: (d ^ b, r, z)) for b in (4, 8, 16, 32) if b < n_dp]

    def local(
        tokens,
        segment_ids,
        doc_starts,
        norm1_gain,
        norm2_gain,
        query_key_value_weight,
        output_weight,
        w_gate_up,
        w_down,
        cotangent,
    ):
        tok_count, width = tokens.shape
        dpi = lax.axis_index("dp")
        row = lax.axis_index("row")
        column = lax.axis_index("col")
        core = dpi % 2
        ybit = (dpi // 2) % 2
        quarter = 2 * ybit + row
        diag = core == row
        heads = query_key_value_weight.shape[1]
        q_heads = heads * GROUP
        q_width = GROUP * HEAD_WIDTH
        shard_rows = w_down.shape[0]
        hidden_width = w_down.shape[1]
        seq_len = min(SEQ_CAP, tok_count * n_col)
        per_seq = seq_len // tok_count
        shard = column % per_seq
        seq_index = column // per_seq
        halo = LEAD + tok_count
        near_to = mover(lambda d, r, z: (d, r, z + 1) if z % per_seq + 1 < per_seq else None)
        far_to = mover(lambda d, r, z: (d, r, z + 2) if z % per_seq == 1 else None)
        near_back = mover(lambda d, r, z: (d, r, z - 1) if z % per_seq >= 1 else None)
        far_back = mover(lambda d, r, z: (d, r, z - 2) if z % per_seq == 3 else None)

        def same_chip(value):
            return jnp.where(diag, value, diag_to_core(value))

        def pick(array, index, axis):
            return lax.dynamic_index_in_dim(array, index, axis, keepdims=False)

        whole_numbers = same_chip(jnp.concatenate([segment_ids, doc_starts.reshape(-1)]))
        tokens_here = same_chip(tokens)
        segment_here = whole_numbers[:tok_count]
        starts_here = whole_numbers[tok_count:].reshape(doc_starts.shape)

        qkv_shard = jnp.concatenate(
            [
                query_key_value_weight[:, :, q_width:].reshape(shard_rows, heads * 128),
                query_key_value_weight[:, :, :q_width].reshape(shard_rows, heads * q_width),
                jnp.zeros((shard_rows, -(heads * (128 + q_width)) % 128), BF),
            ],
            axis=1,
        )
        features = qkv_shard.shape[1]
        part = shard_rows // 4
        quarters = qkv_shard.reshape(4, part, features)
        piece = jnp.where(diag, pick(quarters, quarter, 0), diag_to_x(pick(quarters, quarter ^ 1, 0)))
        pieces = [piece] + [to_z[step](piece) for step in range(1, n_col)]
        rows_z = []
        for z in range(n_col):
            block = pieces[0]
            for step in range(1, n_col):
                block = jnp.where((column - step) % n_col == z, pieces[step], block)
            rows_z.append(block)
        mine = jnp.stack(rows_z)
        from_x = to_x(mine)
        from_y = to_y(mine)
        half_z = n_col // 2
        from_xy = jnp.concatenate([to_y(from_x[:half_z]), to_x(from_y[half_z:])], axis=0)
        by_offset = (mine, from_x, from_y, from_xy)
        blocks = []
        for index in range(4):
            block = by_offset[0]
            for other in range(1, 4):
                block = jnp.where(quarter ^ other == index, by_offset[other], block)
            blocks.append(block)
        full_qkv = jnp.stack(blocks, axis=1).reshape(n_col * shard_rows, features)

        gains = jnp.stack([norm1_gain, norm2_gain])
        gain_parts = [gains] + [to_z[step](gains) for step in range(1, n_col)]
        gain_rows = []
        for z in range(n_col):
            block = gain_parts[0]
            for step in range(1, n_col):
                block = jnp.where((column - step) % n_col == z, gain_parts[step], block)
            gain_rows.append(block)
        gain_all = jnp.concatenate(gain_rows, axis=1).astype(F32)
        gain_one, gain_two = gain_all[0:1], gain_all[1:2]

        order = (0, 2, 1, 3)
        unit = hidden_width // 4

        def units_of(index):
            return jnp.concatenate(
                [
                    lax.dynamic_slice_in_dim(w_gate_up[:, 0], index * unit, unit, 1),
                    lax.dynamic_slice_in_dim(w_gate_up[:, 1], index * unit, unit, 1),
                ],
                axis=1,
            )

        gu_shard = jnp.where(diag, units_of(quarter), diag_to_x(units_of(quarter ^ 1)))
        gu_mine = lax.all_gather(gu_shard, "col", axis=0, tiled=True)
        rest = jnp.concatenate([output_weight.reshape(shard_rows, -1), w_down], axis=1)
        rest = jnp.where(diag, rest, diag_to_x(rest))
        out_features = heads * q_width
        full_out = lax.all_gather(rest[:, :out_features], "col", axis=0, tiled=True)
        down_shard = jnp.concatenate(
            [
                lax.dynamic_slice_in_dim(rest, out_features + (quarter ^ other) * unit, unit, 1)
                for other in order
            ],
            axis=1,
        )
        full_down = lax.all_gather(down_shard, "col", axis=0, tiled=True)
        gu_x = to_x(gu_mine)
        gu_y = to_y(gu_mine)
        half_rows = width // 2
        gu_xy = jnp.concatenate([to_y(gu_x[:half_rows]), to_x(gu_y[half_rows:])], axis=0)
        full_gate_up = jnp.concatenate([gu_mine, gu_y, gu_x, gu_xy], axis=1)

        chosen = jnp.arange(doc_starts.shape[0], dtype=jnp.int32) == seq_index
        start_row = jnp.sum(jnp.where(chosen[:, None], starts_here, 0), axis=0)
        matches = segment_here[:, None] == jnp.arange(doc_starts.shape[1], dtype=jnp.int32)[None, :]
        begins = jnp.sum(jnp.where(matches, start_row[None, :], 0), axis=1)
        in_seq = shard * tok_count + jnp.arange(tok_count, dtype=jnp.int32)
        live = segment_here >= 0
        lived = jnp.sum(live.astype(jnp.int32)).reshape(1)
        lived_one = near_to(lived)[0]
        lived_two = far_to(lived)[0]
        lived = lived[0]
        pad_from = jnp.where(
            lived > 0,
            shard * tok_count + lived,
            jnp.where(
                lived_one > 0,
                (shard - 1) * tok_count + lived_one,
                (shard - 2) * tok_count + lived_two,
            ),
        )
        begin_key = jnp.where(live, begins, pad_from) - (shard * tok_count - halo)
        low = begin_key[::BQ] // BK
        begin_wide = jnp.broadcast_to(begin_key[:, None], (tok_count, 128))
        cosine, sine = rope_tables((in_seq - begins).astype(F32))
        cos_q = jnp.concatenate([cosine] * 4, axis=1)
        sin_q = jnp.concatenate([-sine, sine] * 2, axis=1)
        flat = jnp.ones((tok_count, HEAD_WIDTH), F32)
        cos_k = jnp.concatenate([cosine, cosine, flat], axis=1)
        sin_k = jnp.concatenate([-sine, sine, 0.0 * flat], axis=1)
        cos_t = jnp.transpose(cos_q[:, :HEAD_WIDTH])
        sin_t = jnp.transpose(sin_q[:, :HEAD_WIDTH])

        input_one, queries, kv_own = project(
            tokens_here, gain_one, full_qkv, (cos_q, sin_q, cos_k, sin_k), q_heads, heads
        )
        kv_near = near_to(kv_own)
        kv_far = far_to(kv_own[tok_count - TAIL :])
        sizes = dict(heads=heads, bq=BQ, bk=BK, lead=LEAD, tail=TAIL)
        context, log_totals = attend(low, queries, kv_own, kv_near, kv_far, begin_wide, **sizes)
        attention = dot(context, full_out, ((1,), (1,)))
        layer_input = tokens_here.astype(F32)
        residual = layer_input + attention + to_core(attention.astype(BF)).astype(F32)
        normed_two, inverse_two = rms_parts(residual)
        input_two = (normed_two * gain_two).astype(BF)
        gate_up = dot(input_two, full_gate_up, ((1,), (0,)))

        cotangent_here = same_chip(cotangent)
        grad_out = cotangent_here.astype(F32) * live.astype(F32)[:, None]
        grad_feed = grad_out.astype(BF)
        grad_hidden = dot(grad_feed, full_down, ((1,), (0,)))
        hidden_parts, back_parts = [], []
        for n in range(4):
            gate_value = gate_up[:, 2 * n * unit : (2 * n + 1) * unit]
            up_value = gate_up[:, (2 * n + 1) * unit : (2 * n + 2) * unit]
            back = grad_hidden[:, n * unit : (n + 1) * unit]
            sigmoid_gate = jax.nn.sigmoid(gate_value)
            gate_act = gate_value * sigmoid_gate
            hidden_parts.append((gate_act * up_value).astype(BF))
            back_parts.append(
                (back * up_value * sigmoid_gate * (1.0 + gate_value * (1.0 - sigmoid_gate))).astype(BF)
            )
            back_parts.append((back * gate_act).astype(BF))
        hidden = jnp.concatenate(hidden_parts, axis=1)
        grad_gate_up = jnp.concatenate(back_parts, axis=1)
        part_two = dot(grad_gate_up, full_gate_up, ((1,), (1,)))
        grad_input_two = part_two + to_core(part_two.astype(BF)).astype(F32)

        feed = dot(hidden, full_down, ((1,), (1,)))
        output_here = (residual + feed + to_core(feed.astype(BF)).astype(F32)).astype(BF)
        layer_output = jnp.where(diag, output_here, diag_to_x(output_here))

        split = 4 * unit
        gu_far = dot(input_two, grad_gate_up[:, split:], ((0,), (0,)), BF)
        gu_near = dot(input_two, grad_gate_up[:, :split], ((0,), (0,)), BF)
        down_part = dot(grad_feed, hidden, ((0,), (0,)), BF)
        down_z = lax.psum_scatter(down_part, "col", scatter_dimension=0, tiled=True)
        gu_half = (gu_near.astype(F32) + to_x(gu_far).astype(F32)).astype(BF)
        gu_quarter = (
            gu_half[:, : 2 * unit].astype(F32) + to_y(gu_half[:, 2 * unit :]).astype(F32)
        ).astype(BF)
        gu_z = lax.psum_scatter(gu_quarter, "col", scatter_dimension=0, tiled=True)

        gain_two_grad = jnp.sum(grad_input_two * normed_two, axis=0)
        grad_residual = grad_out + rms_back(grad_input_two * gain_two, normed_two, inverse_two)
        grad_attention = grad_residual.astype(BF)
        grad_context = dot(grad_attention, full_out, ((1,), (0,)), BF)
        out_part = dot(grad_attention, context, ((0,), (0,)), BF)
        out_z = lax.psum_scatter(out_part, "col", scatter_dimension=0, tiled=True)
        q_parts, own_parts, near_parts, far_parts = [], [], [], []
        for head in range(heads):
            dq, d_own, d_near, d_far = attend_back(
                low,
                queries,
                kv_own,
                kv_near,
                kv_far,
                grad_context,
                context,
                log_totals,
                begin_key[None, :],
                cos_t,
                sin_t,
                head=head,
                **sizes,
            )
            q_parts.append(dq)
            own_parts.append(d_own)
            near_parts.append(near_back(d_near))
            far_parts.append(d_far)
        far = far_back(jnp.concatenate(far_parts, axis=1))
        grad_projected, part_one, part_low = unproject(
            q_parts, own_parts, near_parts, far, cos_k, sin_k, full_qkv
        )
        grad_input_one = part_one + to_core(part_low).astype(F32)
        normed_one, inverse_one = rms_parts(layer_input)
        gain_one_grad = jnp.sum(grad_input_one * normed_one, axis=0)
        input_here = (
            grad_residual + rms_back(grad_input_one * gain_one, normed_one, inverse_one)
        ).astype(BF)
        input_grad = jnp.where(diag, input_here, diag_to_x(input_here)).astype(F32)
        qkv_part = dot(input_one, grad_projected, ((0,), (0,)), BF)
        qkv_z = lax.psum_scatter(qkv_part, "col", scatter_dimension=0, tiled=True)

        def over_groups(value):
            for move in dp_bits:
                value = (value.astype(F32) + move(value).astype(F32)).astype(BF)
            return value

        def finish(value):
            summed = (value.astype(F32) + off_to_x(value).astype(F32)).astype(BF)
            summed = (summed.astype(F32) + to_y(summed).astype(F32)).astype(BF)
            return same_chip(over_groups(summed)).astype(F32)

        down_units = [down_z[:, n * unit : (n + 1) * unit] for n in range(4)]
        down_blocks = []
        for index in range(4):
            block = down_units[0]
            for n in range(1, 4):
                block = jnp.where(quarter ^ order[n] == index, down_units[n], block)
            down_blocks.append(block)
        down_true = jnp.concatenate(down_blocks, axis=1)
        both = finish(jnp.concatenate([out_z, down_true], axis=1))
        out_grad = both[:, :out_features].reshape(output_weight.shape)
        down_grad = both[:, out_features:]

        gu_done = over_groups(gu_z)
        gu_other = off_to_x(gu_done)
        gu_first = jnp.where(row == 0, gu_done, gu_other)
        gu_second = jnp.where(row == 0, gu_other, gu_done)
        gu_pair = jnp.concatenate([gu_first, gu_second], axis=1)
        gu_across = to_y(gu_pair)
        gu_low = jnp.where(ybit == 0, gu_pair, gu_across)
        gu_high = jnp.where(ybit == 0, gu_across, gu_pair)
        gu_all = same_chip(jnp.concatenate([gu_low, gu_high], axis=1)).astype(F32)
        gate_up_grad = jnp.stack(
            [
                jnp.concatenate([gu_all[:, 2 * n * unit : (2 * n + 1) * unit] for n in range(4)], axis=1),
                jnp.concatenate([gu_all[:, (2 * n + 1) * unit : (2 * n + 2) * unit] for n in range(4)], axis=1),
            ],
            axis=1,
        )

        qkv_all = finish(qkv_z)
        kv_features = heads * 128
        qkv_grad = jnp.concatenate(
            [
                qkv_all[:, kv_features : kv_features + heads * q_width].reshape(shard_rows, heads, q_width),
                qkv_all[:, :kv_features].reshape(shard_rows, heads, 128),
            ],
            axis=2,
        )

        gain_sums = jnp.stack([gain_one_grad, gain_two_grad])
        for move in [to_x, to_y] + dp_bits + col_bits:
            gain_sums = gain_sums + move(gain_sums)
        gain_sums = jnp.where(core == 0, gain_sums, even_to_core(gain_sums))
        gain_mine = pick(gain_sums.reshape(2, n_col, shard_rows), column, 1)
        return (
            layer_output,
            input_grad,
            gain_mine[0],
            gain_mine[1],
            qkv_grad,
            out_grad,
            gate_up_grad,
            down_grad,
        )

    return local


def solution(mesh):
    placed = (
        P(("dp", "col"), None),
        P(("dp", "col")),
        P("dp", None),
        P("col"),
        P("col"),
        P("col", "row", None),
        P("col", "row", None),
        P("col", None, "row"),
        P("col", "row"),
        P(("dp", "col"), None),
    )
    return jax.shard_map(
        make_local(mesh.shape["dp"], mesh.shape["row"], mesh.shape["col"]),
        mesh=mesh,
        in_specs=placed,
        out_specs=(
            P(("dp", "col"), None),
            P(("dp", "col"), None),
            P("col"),
            P("col"),
            P("col", "row", None),
            P("col", "row", None),
            P("col", None, "row"),
            P("col", "row"),
        ),
        check_vma=False,
    )
```
